256 devices in a mesh: tm: 32 (over x, y, core), cell: 8 (over z).
Axes of the slice: x: 4, y: 4, z: 8, core: 2. Of those that a mesh axis runs over, the one named last changes fastest.
Arguments:
- anomalies: bfloat16 [96, 2, 16384, 256], P('tm', None, 'cell'), may hold values from -6 to 6
- obs_cells: int32 [96, 256], P('tm', 'cell'), may hold values from 0 to 16383, as said below
- obs_counts: int32 [96, 8], P('tm', 'cell'), may hold values from 16 to 32
- obs_precision: float32 [96, 256], P('tm', 'cell'), may hold values from 0.1 to 1
- inflation: float32 [96], P('tm'), may hold values from 1 to 1.12
Outputs:
- smoothed: bfloat16 [96, 2, 16384, 256], P('tm', None, 'cell')
The draws below stay inside these ranges and needn't reach their ends.
Inputs may be any that keep to these rules, and one draw needn't show every extreme that they name: `obs_cells`: slot k of a window names a cell of the block of 2048 cells that starts at (k // 32) * 2048; two slots may name the same cell.
All inputs are finite; a program needn't handle non-finite values.
Results may differ from the reference program's by a relative error of at most 0.017.
Values may be sent and summed in bfloat16 or wider, within the bound.
No kernel may reach another device: no remote copies, remote signals or barrier semaphores. Data moves between devices by JAX's collectives and lax.ppermute only.
A program may use at most 128 MiB of HBM per device.

```python
import math
import jax
import jax.numpy as jnp
from jax import lax

M = 256
CELL_DEV = 2048
OBS_DEV = 32
WINDOWS = 96
CELLS = 16384
OBS = 256
N_CELL = 8


def draw_obs_cells(key, part):
    block = jnp.arange(OBS, dtype=jnp.int32) // OBS_DEV
    offsets = jax.random.randint(key, (WINDOWS, OBS), 0, CELL_DEV, dtype=jnp.int32)
    return offsets + block[None, :] * CELL_DEV


def set_ends(entries, rng, low, top_value):
    longest = entries.shape.index(max(entries.shape))
    spots = []
    for shift in (0, 1):
        where = [jax.random.randint(jax.random.fold_in(rng, axis), (), 0, length) for axis, length in enumerate(entries.shape)]
        where[longest] = (where[longest] + shift) % entries.shape[longest]
        spots.append(tuple(where))
    return entries.at[spots[0]].set(low).at[spots[1]].set(top_value)


def level_of(stream_key, dims, pieces, smallest, high):
    gain = 1.0
    for position, blocks in pieces:
        heights = jax.random.uniform(jax.random.fold_in(jax.random.fold_in(stream_key, 6), position), (blocks,), jnp.float32, smallest / len(pieces), high / len(pieces))
        gain = gain * jnp.repeat(jnp.exp(heights), dims[position] // blocks).reshape((-1,) + (1,) * (len(dims) - 1 - position))
    return gain


def normal_values(key, shape, deviation, reach, shards=(), kind=jnp.bfloat16):
    values = deviation * jax.random.normal(key, shape, jnp.float32)
    if shards:
        values = values * level_of(key, shape, shards, -0.22, 0.18)
    return jnp.clip(values, -reach, reach).astype(kind)


def setup_inputs(seed: int = 0) -> dict:
    streams_of = jax.random.split(jax.random.key(seed), 6)
    anomalies = normal_values(streams_of[0], (WINDOWS, 2, CELLS, M), 1.0, 6.0, ((0, 32), (2, 8)))
    obs_cells = draw_obs_cells(jax.random.fold_in(streams_of[5], 71), 0)
    obs_counts = set_ends(jax.random.randint(streams_of[2], (WINDOWS, N_CELL), OBS_DEV // 2, OBS_DEV + 1), jax.random.fold_in(streams_of[2], 1), OBS_DEV // 2, OBS_DEV).astype(jnp.int32)
    obs_precision = jnp.clip(jnp.exp(math.log(1.0) - 2.3025851 * jax.random.uniform(streams_of[3], (WINDOWS, OBS), jnp.float32) ** level_of(streams_of[3], (WINDOWS, OBS), ((0, 32), (1, 8)), -0.2, 0.2)), 0.1, 1.0)
    inflation = jnp.clip(jnp.exp(math.log(1.12) - 0.11332869 * jax.random.uniform(streams_of[4], (WINDOWS,), jnp.float32) ** level_of(streams_of[4], (WINDOWS,), ((0, 32),), -0.2, 0.2)), 1.0, 1.12)
    return {"anomalies": anomalies, "obs_cells": obs_cells, "obs_counts": obs_counts, "obs_precision": obs_precision, "inflation": inflation}


def one_transform(packed):
    field, cells, counts_row, precision, rho = packed
    picked = field[0][cells].astype(jnp.float32)
    slot = jnp.arange(OBS) % OBS_DEV
    block = jnp.arange(OBS) // OBS_DEV
    live = slot < counts_row[block]
    weights = jnp.where(live, precision, jnp.float32(0.0))
    weighted = picked * weights[:, None]
    gram = jnp.dot(weighted.T.astype(jnp.float32), picked.astype(jnp.float32), precision=lax.Precision.HIGHEST, preferred_element_type=jnp.float32)
    unit_matrix = jnp.eye(M, dtype=jnp.float32)
    system = (M - 1.0) * unit_matrix + gram
    factor = jnp.linalg.cholesky(system)
    inverse = jax.scipy.linalg.solve_triangular(factor, unit_matrix, lower=True)
    return rho * jnp.sqrt(jnp.float32(M - 1.0)) * inverse.T

def reference(anomalies, obs_cells, obs_counts, obs_precision, inflation):
    transforms = lax.map(one_transform, (anomalies, obs_cells, obs_counts, obs_precision, inflation))

    def backward(carried, current):
        product = jnp.dot(current.astype(jnp.float32), carried.astype(jnp.float32), precision=lax.Precision.HIGHEST, preferred_element_type=jnp.float32)
        return (product, product)
    unit_matrix = jnp.eye(M, dtype=jnp.float32)
    _, suffixes = lax.scan(backward, unit_matrix, transforms, reverse=True)
    weights = suffixes.astype(jnp.bfloat16)

    def apply_window(packed):
        field, weight_matrix = packed
        flat = field.reshape(2 * CELLS, M)
        result = jnp.dot(flat.astype(jnp.float32), weight_matrix.astype(jnp.float32), preferred_element_type=jnp.float32)
        return result.astype(jnp.bfloat16).reshape(2, CELLS, M)
    return lax.map(apply_window, (anomalies, weights))
```

```python
import functools
import math
import jax
import jax.numpy as jnp
from jax import lax
from jax.experimental import pallas as pl
from jax.experimental.pallas import tpu as pltpu
from jax.sharding import Mesh
from jax.sharding import PartitionSpec as P

TM = ("tm_0", "tm_1", "tm_2")
VMEM = pltpu.VMEM
F32 = jnp.float32
BF16 = jnp.bfloat16
HI = lax.Precision.HIGHEST
B = 32
T = 8


def dot(a, b, precision=None):
    return jnp.dot(a, b, precision=precision, preferred_element_type=F32)


def dot_nt(a, b, precision=None):
    return lax.dot_general(a, b, (((1,), (1,)), ((), ())), precision=precision, preferred_element_type=F32)


def dot_tn(a, b, precision=None):
    return lax.dot_general(a, b, (((0,), (0,)), ((), ())), precision=precision, preferred_element_type=F32)


def split3(v):
    hi = v.astype(BF16)
    rest = v - hi.astype(F32)
    mid = rest.astype(BF16)
    lo = (rest - mid.astype(F32)).astype(BF16)
    return hi, mid, lo


def dot_x3(a, b):
    ah = a.astype(BF16)
    al = (a - ah.astype(F32)).astype(BF16)
    bh = b.astype(BF16)
    bl = (b - bh.astype(F32)).astype(BF16)
    return dot(ah, bh) + (dot(ah, bl) + dot(al, bh))


def row_of(tile, i):
    return jnp.broadcast_to(tile[i : i + 1, :], tile.shape)


def inverse_factors(tiles, lane):
    n = len(tiles)
    sub = lax.broadcasted_iota(jnp.int32, (T, 128), 0)
    base = (lane // B) * B
    local = lane - base
    roots = []
    for t in range(n):
        cols = []
        for i in range(T):
            index = base + (t * T + i)
            cols.append([jnp.take_along_axis(tiles[r], index, axis=1) if r >= t else None for r in range(n)])
        pivots = []
        for i in range(T):
            j = t * T + i
            pivot = row_of(cols[i][t], i)
            inv = 1.0 / pivot
            pivots.append(pivot)
            here = local == j
            row = jnp.where(here, 1.0, row_of(tiles[t], i)) * inv
            follow = [row_of(cols[m][t], i) * inv for m in range(i + 1, T)]
            for r in range(t, n):
                c = cols[i][r]
                if r == t:
                    c = jnp.where(sub > i, c, 0.0)
                    keep = jnp.where(here & (sub > i), 0.0, tiles[r])
                    keep = jnp.where(here & (sub == i), 1.0, keep)
                else:
                    keep = jnp.where(here, 0.0, tiles[r])
                tiles[r] = keep - c * row
                for m in range(i + 1, T):
                    cols[m][r] = cols[m][r] - c * follow[m - i - 1]
        d = pivots[0]
        for i in range(1, T):
            d = jnp.where(sub == i, pivots[i], d)
        roots.append(lax.rsqrt(d))
    out = []
    for t in range(n):
        low = local <= (sub + t * T)
        out.append(jnp.where(low, tiles[t] * roots[t], 0.0))
    return out


def factor_body(nwin, gram_of_window, X):
    nb = 256 // B
    lane = lax.broadcasted_iota(jnp.int32, (T, 128), 1)
    lane_b = lax.broadcasted_iota(jnp.int32, (B, 128), 1)
    lane_r = lax.broadcasted_iota(jnp.int32, (B, 256), 1)
    rows_b = lax.broadcasted_iota(jnp.int32, (B, 256), 0)
    for w in range(nwin):
        g = gram_of_window(w)
        for k in range(nb):
            X[k, w * B : (w + 1) * B, :] = g[k * B : (k + 1) * B, :] + jnp.where(lane_r == rows_b + k * B, 255.0, 0.0)
    for k in range(nb):
        half = (k * B) // 128
        at = (k * B) % 128
        tiles = []
        for t in range(B // T):
            tile = None
            for w in range(nwin):
                part = X[k, w * B + t * T : w * B + (t + 1) * T, half * 128 : half * 128 + 128]
                shift = (w * B - at) % 128
                if shift:
                    part = pltpu.roll(part, shift, 1)
                tile = part if w == 0 else jnp.where(lane >= w * B, part, tile)
            tiles.append(tile)
        inv = jnp.concatenate(inverse_factors(tiles, lane), axis=0)
        diag = jnp.concatenate([jnp.where(lane_b // B == w, inv, 0.0) for w in range(nwin)], axis=0)
        rows = X[k]
        q = dot(diag[:, : nwin * B], rows, HI)
        lane_q = lax.broadcasted_iota(jnp.int32, (B, 256), 1)
        inside = (lane_q >= k * B) & (lane_q < (k + 1) * B)
        qs = []
        for w in range(nwin):
            shift = (at - w * B) % 128
            moved = jnp.where(lane_b // B == w, inv, 0.0)
            if shift:
                moved = pltpu.roll(moved, shift, 1)
            zero = jnp.zeros((B, 128), F32)
            wide = jnp.concatenate([moved, zero] if half == 0 else [zero, moved], axis=1)
            qw = jnp.where(inside, wide, q[w * B : (w + 1) * B])
            qs.append((qw, moved))
            X[k, w * B : (w + 1) * B, :] = jnp.where(lane_q < (k + 1) * B, qw, 0.0)
        for w in range(nwin):
            qw, moved = qs[w]
            if k + 1 == nb:
                continue
            below = X[k + 1 :, w * B : (w + 1) * B, :]
            nrow = (nb - k - 1) * B
            p = dot_nt(below[:, :, half * 128 : half * 128 + 128].reshape(nrow, 128), moved, HI)
            upd = dot(p, qw, HI).reshape(nb - k - 1, B, 256)
            X[k + 1 :, w * B : (w + 1) * B, :] = jnp.where(inside[None], 0.0, below) - upd


def factor_kernel(g_ref, scale_ref, part_ref, own_ref, X, Y):
    nz = g_ref.shape[0]
    nwin = scale_ref.shape[0]
    slots = 32
    packed = []
    for z in range(nz):
        both = g_ref[z, nwin * slots : nwin * slots + 8, :].astype(F32)
        packed.append((both[:, :128] + both[:, 128:]))
    columns = jnp.concatenate(packed, axis=0)
    columns = jnp.concatenate([columns, columns], axis=0).T

    def gram(w):
        parts = []
        for z in range(nz):
            y = g_ref[z, w * slots : (w + 1) * slots, :]
            Y[w, z * slots : (z + 1) * slots, :] = y
            col = columns[:slots, z * 8 + w : z * 8 + w + 1]
            parts.append(y.astype(F32) * col)
        weighted = jnp.concatenate(parts, axis=0)
        hi, mid, lo = split3(weighted)
        y = Y[w].T
        return dot(y, hi) + (dot(y, mid) + dot(y, lo))

    factor_body(nwin, gram, X)
    s = None
    for w in reversed(range(nwin)):
        x = X[:, w * B : (w + 1) * B, :].reshape(256, 256) * scale_ref[w]
        s = x if s is None else dot_x3(s, x)
        part_ref[w] = s
    own_ref[...] = s.astype(BF16)


def factor_call(g, scale):
    nwin = scale.shape[0]
    return pl.pallas_call(
        factor_kernel,
        in_specs=[pl.BlockSpec(memory_space=pltpu.VMEM), pl.BlockSpec(memory_space=pltpu.SMEM)],
        out_specs=[pl.BlockSpec(memory_space=pltpu.VMEM)] * 2,
        out_shape=[jax.ShapeDtypeStruct((nwin, 256, 256), F32), jax.ShapeDtypeStruct((256, 256), BF16)],
        scratch_shapes=[pltpu.VMEM((256 // B, nwin * B, 256), F32), pltpu.VMEM((nwin, 256, 256), BF16)],
        name="factor",
    )(g, scale)


WHOLE = pl.BlockSpec(memory_space=pltpu.VMEM)
SCALARS = pl.BlockSpec(memory_space=pltpu.SMEM)


def pick_kernel(cells_ref, counts_ref, precision_ref, field_ref, out_ref, near, row_scr, sem):
    nwin, slots = cells_ref.shape
    width = field_ref.shape[2]

    def copy_of(w, k):
        offset = lax.rem(cells_ref[w, k], width)
        first = pl.multiple_of((offset // 16) * 16, 16)
        return pltpu.make_async_copy(field_ref.at[w, 0, pl.ds(first, 16), :], near.at[w * slots + k], sem)

    for w in range(nwin):
        for k in range(slots):
            copy_of(w, k).start()
    row_scr[...] = jnp.zeros(row_scr.shape, F32)
    lane = lax.broadcasted_iota(jnp.int32, (1, slots), 1)
    for w in range(nwin):
        row_scr[w : w + 1, :slots] = jnp.where(lane < counts_ref[w, 0], precision_ref[w : w + 1, :], 0.0)
    live = row_scr[...]
    high = live.astype(BF16)
    low = (live - high.astype(F32)).astype(BF16)
    tail = jnp.concatenate([high, low], axis=1)
    pltpu.make_async_copy(near, near, sem).wait()
    sub = lax.broadcasted_iota(jnp.int32, (16, 256), 0)
    rows = []
    for w in range(nwin):
        for k in range(slots):
            within = lax.rem(cells_ref[w, k], 16)
            tile = near[w * slots + k].astype(F32)
            rows.append(jnp.sum(jnp.where(sub == within, tile, 0.0), axis=0, keepdims=True))
    for w in range(nwin):
        block = jnp.concatenate(rows[w * slots : (w + 1) * slots], axis=0).astype(BF16)
        for z in range(out_ref.shape[0]):
            out_ref[z, w * slots : (w + 1) * slots, :] = block
    for z in range(out_ref.shape[0]):
        out_ref[z, nwin * slots :, :] = tail


def pick_call(copies, anomalies, obs_cells, obs_counts, obs_precision):
    nwin, slots = obs_cells.shape
    members = anomalies.shape[3]
    return pl.pallas_call(
        pick_kernel,
        in_specs=[SCALARS, SCALARS, WHOLE, pl.BlockSpec(memory_space=pl.ANY)],
        out_specs=WHOLE,
        out_shape=jax.ShapeDtypeStruct((copies, nwin * slots + 8, members), BF16),
        scratch_shapes=[
            pltpu.VMEM((nwin * slots, 16, members), BF16),
            pltpu.VMEM((8, 128), F32),
            pltpu.SemaphoreType.DMA,
        ],
        name="pick",
    )(obs_cells, obs_counts, obs_precision, anomalies)


def identity_bf16(n):
    return (lax.broadcasted_iota(jnp.int32, (n, n), 0) == lax.broadcasted_iota(jnp.int32, (n, n), 1)).astype(BF16)


def pair_kernel(mine_ref, other_ref, both_ref):
    core = lax.axis_index("tm_2")
    first = jnp.where(core == 0, mine_ref[...].astype(F32), other_ref[...].astype(F32)).astype(BF16)
    second = jnp.where(core == 0, other_ref[...].astype(F32), mine_ref[...].astype(F32)).astype(BF16)
    both_ref[...] = dot(second, first).astype(BF16)


def later_of(q, me):
    return [lambda: dot_x3(dot(q[3], q[2]), q[1].astype(F32)), lambda: dot(q[3], q[2]), lambda: q[3].astype(F32)]


def ring_kernel(p0, p1, p2, p3, total_ref, later_ref, q):
    me = lax.axis_index("tm_1")
    for s, piece in enumerate((p0, p1, p2, p3)):
        q[lax.rem(me + s, 4)] = piece[...]
    high = dot(q[3], q[2])
    total_ref[...] = dot_x3(high, dot(q[1], q[0])).astype(BF16)
    later_ref[...] = high

    @pl.when(me == 0)
    def _():
        later_ref[...] = dot_x3(high, q[1].astype(F32))

    @pl.when(me == 2)
    def _():
        later_ref[...] = q[3].astype(F32)

    @pl.when(me == 3)
    def _():
        later_ref[...] = identity_bf16(256).astype(F32)


def inner_kernel(later_ref, other_ref, part_ref, out_ref, before):
    core = lax.axis_index("tm_2")
    before[...] = later_ref[...]

    @pl.when(core == 0)
    def _():
        before[...] = dot_x3(later_ref[...], other_ref[...].astype(F32))

    for w in range(part_ref.shape[0]):
        out_ref[w] = dot_x3(before[...], part_ref[w])


def apply_kernel(p1, p2, p3, inner_ref, field_ref, out_ref, q, later, weights):
    @pl.when((pl.program_id(0) == 0) & (pl.program_id(1) == 0))
    def _():
        me = lax.axis_index("tm_0")
        for s, piece in enumerate((p1, p2, p3)):
            q[lax.rem(me + s + 1, 4)] = piece[...]

        @pl.when(me == 0)
        def _():
            later[...] = dot_x3(dot(q[3], q[2]), q[1].astype(F32))

        @pl.when(me == 1)
        def _():
            later[...] = dot(q[3], q[2])

        @pl.when(me == 2)
        def _():
            later[...] = q[3].astype(F32)

        @pl.when(me == 3)
        def _():
            later[...] = identity_bf16(256).astype(F32)

        for w in range(inner_ref.shape[0]):
            weights[w] = dot_x3(later[...], inner_ref[w]).astype(BF16)

    out_ref[0] = dot_nt(field_ref[0], weights[pl.program_id(0)]).astype(BF16)


def apply_call(pieces, inner, flat):
    nwin, rows, members = flat.shape
    step = 1024
    block = pl.BlockSpec((1, step, members), lambda w, i: (w, i, 0))
    return pl.pallas_call(
        apply_kernel,
        grid=(nwin, rows // step),
        in_specs=[WHOLE] * 4 + [block],
        out_specs=block,
        out_shape=jax.ShapeDtypeStruct(flat.shape, BF16),
        scratch_shapes=[
            pltpu.VMEM((4, members, members), BF16),
            pltpu.VMEM((members, members), F32),
            pltpu.VMEM((nwin, members, members), BF16),
        ],
        name="apply",
    )(*pieces, inner, flat)


def simple_call(kernel, name, out_shape, scratch, *args):
    return pl.pallas_call(
        kernel,
        in_specs=[WHOLE] * len(args),
        out_specs=jax.tree.map(lambda _: WHOLE, out_shape),
        out_shape=out_shape,
        scratch_shapes=scratch,
        name=name,
    )(*args)


def from_after(array, axis, shift):
    count = lax.axis_size(axis)
    return lax.ppermute(array, axis, [(i, (i - shift) % count) for i in range(count)])


def local(anomalies, obs_cells, obs_counts, obs_precision, inflation):
    nwin, _, cell_width, members = anomalies.shape
    square = (members, members)
    sent = pick_call(lax.axis_size("cell"), anomalies, obs_cells, obs_counts, obs_precision)
    gathered = lax.all_to_all(sent, "cell", split_axis=0, concat_axis=0, tiled=True)
    part, own = factor_call(gathered, inflation * math.sqrt(members - 1.0))
    other = from_after(own, "tm_2", 1)
    both = simple_call(pair_kernel, "pair", jax.ShapeDtypeStruct(square, BF16), [], own, other)
    pieces = [both] + [from_after(both, "tm_1", s) for s in (1, 2, 3)]
    total, later = simple_call(
        ring_kernel,
        "ring",
        [jax.ShapeDtypeStruct(square, BF16), jax.ShapeDtypeStruct(square, F32)],
        [pltpu.VMEM((4, *square), BF16)],
        *pieces,
    )
    after = [from_after(total, "tm_0", s) for s in (1, 2, 3)]
    inner = simple_call(
        inner_kernel,
        "inner",
        jax.ShapeDtypeStruct((nwin, *square), F32),
        [pltpu.VMEM(square, F32)],
        later,
        other,
        part,
    )
    flat = anomalies.reshape(nwin, 2 * cell_width, members)
    return apply_call(after, inner, flat).reshape(anomalies.shape)


def solution(mesh):
    torus = Mesh(
        mesh.devices.reshape(4, 4, 2, mesh.shape["cell"]), ("tm_0", "tm_1", "tm_2", "cell")
    )
    return jax.shard_map(
        local,
        mesh=torus,
        in_specs=(P(TM, None, "cell", None), P(TM, "cell"), P(TM, "cell"), P(TM, "cell"), P(TM)),
        out_specs=P(TM, None, "cell", None),
        check_vma=False,
    )
```

```python
import functools
import math
import jax
import jax.numpy as jnp
from jax import lax
from jax.experimental import pallas as pl
from jax.experimental.pallas import tpu as pltpu
from jax.sharding import Mesh
from jax.sharding import PartitionSpec as P

TM = ("tm_0", "tm_1", "tm_2")
WHOLE = pl.BlockSpec(memory_space=pltpu.VMEM)
SCALARS = pl.BlockSpec(memory_space=pltpu.SMEM)
F32 = jnp.float32
BF16 = jnp.bfloat16
HI = lax.Precision.HIGHEST
B = 32
T = 8


def dot(a, b, precision=None):
    return jnp.dot(a, b, precision=precision, preferred_element_type=F32)


def dot_nt(a, b, precision=None):
    return lax.dot_general(a, b, (((1,), (1,)), ((), ())), precision=precision, preferred_element_type=F32)


def dot_tn(a, b, precision=None):
    return lax.dot_general(a, b, (((0,), (0,)), ((), ())), precision=precision, preferred_element_type=F32)


def split3(v):
    hi = v.astype(BF16)
    rest = v - hi.astype(F32)
    mid = rest.astype(BF16)
    lo = (rest - mid.astype(F32)).astype(BF16)
    return hi, mid, lo


def dot_x3(a, b):
    ah = a.astype(BF16)
    al = (a - ah.astype(F32)).astype(BF16)
    bh = b.astype(BF16)
    bl = (b - bh.astype(F32)).astype(BF16)
    return dot(ah, bh) + (dot(ah, bl) + dot(al, bh))


def row_of(tile, i):
    return jnp.broadcast_to(tile[i : i + 1, :], tile.shape)


def inverse_factors(tiles, lane):
    n = len(tiles)
    sub = lax.broadcasted_iota(jnp.int32, (T, 128), 0)
    base = (lane // B) * B
    local = lane - base
    roots = []
    for t in range(n):
        cols = []
        for i in range(T):
            index = base + (t * T + i)
            cols.append([jnp.take_along_axis(tiles[r], index, axis=1) if r >= t else None for r in range(n)])
        pivots = []
        for i in range(T):
            j = t * T + i
            pivot = row_of(cols[i][t], i)
            inv = 1.0 / pivot
            pivots.append(pivot)
            here = local == j
            row = jnp.where(here, 1.0, row_of(tiles[t], i)) * inv
            follow = [row_of(cols[m][t], i) * inv for m in range(i + 1, T)]
            for r in range(t, n):
                c = cols[i][r]
                if r == t:
                    c = jnp.where(sub > i, c, 0.0)
                    keep = jnp.where(here & (sub > i), 0.0, tiles[r])
                    keep = jnp.where(here & (sub == i), 1.0, keep)
                else:
                    keep = jnp.where(here, 0.0, tiles[r])
                tiles[r] = keep - c * row
                for m in range(i + 1, T):
                    cols[m][r] = cols[m][r] - c * follow[m - i - 1]
        d = pivots[0]
        for i in range(1, T):
            d = jnp.where(sub == i, pivots[i], d)
        roots.append(lax.rsqrt(d))
    out = []
    for t in range(n):
        low = local <= (sub + t * T)
        out.append(jnp.where(low, tiles[t] * roots[t], 0.0))
    return out


def factor_body(nwin, gram_of_window, X):
    nb = 256 // B
    lane = lax.broadcasted_iota(jnp.int32, (T, 128), 1)
    lane_b = lax.broadcasted_iota(jnp.int32, (B, 128), 1)
    lane_r = lax.broadcasted_iota(jnp.int32, (B, 256), 1)
    rows_b = lax.broadcasted_iota(jnp.int32, (B, 256), 0)
    for w in range(nwin):
        g = gram_of_window(w)
        for k in range(nb):
            X[k, w * B : (w + 1) * B, :] = g[k * B : (k + 1) * B, :] + jnp.where(lane_r == rows_b + k * B, 255.0, 0.0)
    for k in range(nb):
        half = (k * B) // 128
        at = (k * B) % 128
        tiles = []
        for t in range(B // T):
            tile = None
            for w in range(nwin):
                part = X[k, w * B + t * T : w * B + (t + 1) * T, half * 128 : half * 128 + 128]
                shift = (w * B - at) % 128
                if shift:
                    part = pltpu.roll(part, shift, 1)
                tile = part if w == 0 else jnp.where(lane >= w * B, part, tile)
            tiles.append(tile)
        inv = jnp.concatenate(inverse_factors(tiles, lane), axis=0)
        diag = jnp.concatenate([jnp.where(lane_b // B == w, inv, 0.0) for w in range(nwin)], axis=0)
        rows = X[k]
        q = dot(diag[:, : nwin * B], rows, HI)
        lane_q = lax.broadcasted_iota(jnp.int32, (B, 256), 1)
        inside = (lane_q >= k * B) & (lane_q < (k + 1) * B)
        qs = []
        for w in range(nwin):
            shift = (at - w * B) % 128
            moved = jnp.where(lane_b // B == w, inv, 0.0)
            if shift:
                moved = pltpu.roll(moved, shift, 1)
            zero = jnp.zeros((B, 128), F32)
            wide = jnp.concatenate([moved, zero] if half == 0 else [zero, moved], axis=1)
            qw = jnp.where(inside, wide, q[w * B : (w + 1) * B])
            qs.append(qw)
            X[k, w * B : (w + 1) * B, :] = jnp.where(lane_q < (k + 1) * B, qw, 0.0)
        if k + 1 == nb:
            continue
        for w in range(nwin):
            q1, q2, q3 = split3(qs[w])
            start = 128 * ((k + 1) * B // 128)
            left = jnp.concatenate([q1, q1, q1, q2, q2, q3], axis=0)[:, start:].T
            right = jnp.concatenate([q1, q2, q3, q1, q2, q1], axis=0)
            upd = dot(left[(k + 1) * B - start :], right).reshape(nb - k - 1, B, 256)
            below = X[k + 1 :, w * B : (w + 1) * B, :]
            X[k + 1 :, w * B : (w + 1) * B, :] = jnp.where(inside[None], 0.0, below) - upd


def factor_kernel(g_ref, scale_ref, far_ref, part_ref, own_ref, near_ref, X, Y, sem):
    fetch = pltpu.make_async_copy(far_ref, near_ref, sem)
    fetch.start()
    nz = g_ref.shape[0]
    nwin = scale_ref.shape[0]
    slots = 32
    packed = []
    for z in range(nz):
        both = g_ref[z, nwin * slots : nwin * slots + 8, :].astype(F32)
        packed.append((both[:, :128] + both[:, 128:]))
    columns = jnp.concatenate(packed, axis=0)
    columns = jnp.concatenate([columns, columns], axis=0).T

    def gram(w):
        parts = []
        for z in range(nz):
            y = g_ref[z, w * slots : (w + 1) * slots, :]
            Y[w, z * slots : (z + 1) * slots, :] = y
            col = columns[:slots, z * 8 + w : z * 8 + w + 1]
            parts.append(y.astype(F32) * col)
        weighted = jnp.concatenate(parts, axis=0)
        hi, mid, lo = split3(weighted)
        y = Y[w].T
        return dot(y, hi) + (dot(y, mid) + dot(y, lo))

    factor_body(nwin, gram, X)
    s = None
    for w in reversed(range(nwin)):
        x = X[:, w * B : (w + 1) * B, :].reshape(256, 256) * scale_ref[w]
        s = x if s is None else dot_x3(s, x)
        part_ref[w] = s
    own_ref[...] = pack(s).astype(BF16)
    fetch.wait()


def factor_call(g, scale, flat):
    nwin = scale.shape[0]
    return pl.pallas_call(
        factor_kernel,
        in_specs=[WHOLE, SCALARS, pl.BlockSpec(memory_space=pltpu.HBM)],
        out_specs=[WHOLE] * 3,
        out_shape=[
            jax.ShapeDtypeStruct((nwin, 256, 256), F32),
            PACKED,
            pltpu.VMEM(flat.shape, BF16),
        ],
        scratch_shapes=[
            pltpu.VMEM((256 // B, nwin * B, 256), F32),
            pltpu.VMEM((nwin, 256, 256), BF16),
            pltpu.SemaphoreType.DMA,
        ],
        compiler_params=pltpu.CompilerParams(vmem_limit_bytes=12 << 20),
        name="factor",
    )(g, scale, pltpu.with_memory_space_constraint(flat, pltpu.HBM))


def pick_kernel(cells_ref, counts_ref, precision_ref, field_ref, out_ref, near, row_scr, sem):
    nwin, slots = cells_ref.shape
    width = field_ref.shape[2]

    def copy_of(w, k):
        offset = lax.rem(cells_ref[w, k], width)
        first = pl.multiple_of((offset // 16) * 16, 16)
        return pltpu.make_async_copy(field_ref.at[w, 0, pl.ds(first, 16), :], near.at[w * slots + k], sem)

    for w in range(nwin):
        for k in range(slots):
            copy_of(w, k).start()
    row_scr[...] = jnp.zeros(row_scr.shape, F32)
    lane = lax.broadcasted_iota(jnp.int32, (1, slots), 1)
    for w in range(nwin):
        row_scr[w : w + 1, :slots] = jnp.where(lane < counts_ref[w], precision_ref[w : w + 1, :], 0.0)
    live = row_scr[...]
    high = live.astype(BF16)
    low = (live - high.astype(F32)).astype(BF16)
    tail = jnp.concatenate([high, low], axis=1)
    pltpu.make_async_copy(near, near, sem).wait()
    sub = lax.broadcasted_iota(jnp.int32, (16, 256), 0)
    rows = []
    for w in range(nwin):
        for k in range(slots):
            within = lax.rem(cells_ref[w, k], 16)
            tile = near[w * slots + k].astype(F32)
            rows.append(jnp.sum(jnp.where(sub == within, tile, 0.0), axis=0, keepdims=True))
    for w in range(nwin):
        block = jnp.concatenate(rows[w * slots : (w + 1) * slots], axis=0).astype(BF16)
        for z in range(out_ref.shape[0]):
            out_ref[z, w * slots : (w + 1) * slots, :] = block
    for z in range(out_ref.shape[0]):
        out_ref[z, nwin * slots :, :] = tail


def pick_call(copies, anomalies, obs_cells, obs_counts, obs_precision):
    nwin, slots = obs_cells.shape
    members = anomalies.shape[3]
    return pl.pallas_call(
        pick_kernel,
        in_specs=[SCALARS, SCALARS, WHOLE, pl.BlockSpec(memory_space=pltpu.HBM)],
        out_specs=WHOLE,
        out_shape=jax.ShapeDtypeStruct((copies, nwin * slots + 8, members), BF16),
        scratch_shapes=[
            pltpu.VMEM((nwin * slots, 16, members), BF16),
            pltpu.VMEM((8, 128), F32),
            pltpu.SemaphoreType.DMA,
        ],
        name="pick",
    )(obs_cells, obs_counts, obs_precision, pltpu.with_memory_space_constraint(anomalies, pltpu.HBM))


def identity_bf16(n):
    return (lax.broadcasted_iota(jnp.int32, (n, n), 0) == lax.broadcasted_iota(jnp.int32, (n, n), 1)).astype(BF16)


def pack(s):
    h = 64
    top = jnp.concatenate([s[:h, :128][:, :h], s[128 : 128 + h, 128:][:, :h]], axis=1)
    return jnp.concatenate([top, s[h:128, :128], s[128 + h :, 128:], s[128:, :128]], axis=0)


def unpack(p):
    h = 64
    zero = jnp.zeros((h, h), p.dtype)
    first = jnp.concatenate([jnp.concatenate([p[:h, :h], zero], axis=1), p[h : 2 * h]], axis=0)
    last = jnp.concatenate([jnp.concatenate([p[:h, h:], zero], axis=1), p[2 * h : 3 * h]], axis=0)
    upper = jnp.concatenate([first, jnp.zeros((128, 128), p.dtype)], axis=1)
    lower = jnp.concatenate([p[3 * h :], last], axis=1)
    return jnp.concatenate([upper, lower], axis=0)


PACKED = jax.ShapeDtypeStruct((320, 128), jnp.bfloat16)


def pair_kernel(mine_ref, other_ref, both_ref):
    core = lax.axis_index("tm_2")
    mine, other = mine_ref[...].astype(F32), other_ref[...].astype(F32)
    first = unpack(jnp.where(core == 0, mine, other)).astype(BF16)
    second = unpack(jnp.where(core == 0, other, mine)).astype(BF16)
    both_ref[...] = pack(dot(second, first)).astype(BF16)


def ring_kernel(p0, p1, p2, p3, total_ref, later_ref, q):
    me = lax.axis_index("tm_1")
    for s, piece in enumerate((p0, p1, p2, p3)):
        q[lax.rem(me + s, 4)] = unpack(piece[...].astype(F32)).astype(BF16)
    high = dot(q[3], q[2])
    total_ref[...] = pack(dot_x3(high, dot(q[1], q[0]))).astype(BF16)
    later_ref[...] = high

    @pl.when(me == 0)
    def _():
        later_ref[...] = dot_x3(high, q[1].astype(F32))

    @pl.when(me == 2)
    def _():
        later_ref[...] = q[3].astype(F32)

    @pl.when(me == 3)
    def _():
        later_ref[...] = identity_bf16(256).astype(F32)


def inner_kernel(later_ref, other_ref, part_ref, out_ref, before):
    core = lax.axis_index("tm_2")
    before[...] = later_ref[...]

    @pl.when(core == 0)
    def _():
        before[...] = dot_x3(later_ref[...], unpack(other_ref[...].astype(F32)))

    for w in range(part_ref.shape[0]):
        out_ref[w] = dot_x3(before[...], part_ref[w])


def apply_kernel(p1, p2, p3, inner_ref, field_ref, out_ref, q, later, result, sems):
    me = lax.axis_index("tm_0")
    for s, piece in enumerate((p1, p2, p3)):
        q[lax.rem(me + s + 1, 4)] = unpack(piece[...].astype(F32)).astype(BF16)

    @pl.when(me == 0)
    def _():
        later[...] = dot_x3(dot(q[3], q[2]), q[1].astype(F32))

    @pl.when(me == 1)
    def _():
        later[...] = dot(q[3], q[2])

    @pl.when(me == 2)
    def _():
        later[...] = q[3].astype(F32)

    @pl.when(me == 3)
    def _():
        later[...] = identity_bf16(256).astype(F32)

    nwin, rows, _ = field_ref.shape
    copies = []
    for w in range(nwin):
        weights = dot_x3(later[...], inner_ref[w]).T.astype(BF16)
        for half in range(STEPS):
            span = pl.ds(half * (rows // STEPS), rows // STEPS)
            result[w, span, :] = dot(field_ref[w, span, :], weights).astype(BF16)
            copy = pltpu.make_async_copy(result.at[w, span], out_ref.at[w, span], sems.at[w, half])
            copy.start()
            copies.append(copy)
    for copy in copies:
        copy.wait()


STEPS = 2


def apply_call(pieces, inner, flat):
    nwin, rows, members = flat.shape
    return pl.pallas_call(
        apply_kernel,
        in_specs=[WHOLE] * 5,
        out_specs=pl.BlockSpec(memory_space=pltpu.HBM),
        out_shape=jax.ShapeDtypeStruct(flat.shape, BF16),
        scratch_shapes=[
            pltpu.VMEM((4, members, members), BF16),
            pltpu.VMEM((members, members), F32),
            pltpu.VMEM(flat.shape, BF16),
            pltpu.SemaphoreType.DMA((nwin, STEPS)),
        ],
        compiler_params=pltpu.CompilerParams(vmem_limit_bytes=24 << 20),
        name="apply",
    )(*pieces, inner, flat)


def simple_call(kernel, name, out_shape, scratch, *args):
    return pl.pallas_call(
        kernel,
        in_specs=[WHOLE] * len(args),
        out_specs=jax.tree.map(lambda _: WHOLE, out_shape),
        out_shape=out_shape,
        scratch_shapes=scratch,
        compiler_params=pltpu.CompilerParams(vmem_limit_bytes=8 << 20),
        name=name,
    )(*args)


def from_after(array, axis, shift):
    count = lax.axis_size(axis)
    return lax.ppermute(array, axis, [(i, (i - shift) % count) for i in range(count)])


def local(anomalies, obs_cells, obs_counts, obs_precision, inflation):
    nwin, _, cell_width, members = anomalies.shape
    square = (members, members)
    sent = pick_call(lax.axis_size("cell"), anomalies, obs_cells, obs_counts.reshape(nwin), obs_precision)
    flat = anomalies.reshape(nwin, 2 * cell_width, members)
    gathered = lax.all_to_all(sent, "cell", split_axis=0, concat_axis=0, tiled=True)
    part, own, near = factor_call(gathered, inflation * math.sqrt(members - 1.0), flat)
    other = from_after(own, "tm_2", 1)
    both = simple_call(pair_kernel, "pair", PACKED, [], own, other)
    pieces = [both] + [from_after(both, "tm_1", s) for s in (1, 2, 3)]
    total, later = simple_call(
        ring_kernel,
        "ring",
        [PACKED, jax.ShapeDtypeStruct(square, F32)],
        [pltpu.VMEM((4, *square), BF16)],
        *pieces,
    )
    after = [from_after(total, "tm_0", s) for s in (1, 2, 3)]
    inner = simple_call(
        inner_kernel,
        "inner",
        jax.ShapeDtypeStruct((nwin, *square), F32),
        [pltpu.VMEM(square, F32)],
        later,
        other,
        part,
    )
    return apply_call(after, inner, near).reshape(anomalies.shape)


def solution(mesh):
    torus = Mesh(
        mesh.devices.reshape(4, 4, 2, mesh.shape["cell"]), ("tm_0", "tm_1", "tm_2", "cell")
    )
    return jax.shard_map(
        local,
        mesh=torus,
        in_specs=(P(TM, None, "cell", None), P(TM, "cell"), P(TM, "cell"), P(TM, "cell"), P(TM)),
        out_specs=P(TM, None, "cell", None),
        check_vma=False,
    )
```

```python
import functools
import math
import jax
import jax.numpy as jnp
from jax import lax
from jax.experimental import pallas as pl
from jax.experimental.pallas import tpu as pltpu
from jax.sharding import Mesh
from jax.sharding import PartitionSpec as P

TM = ("tm_0", "tm_1", "tm_2")
WHOLE = pl.BlockSpec(memory_space=pltpu.VMEM)
SCALARS = pl.BlockSpec(memory_space=pltpu.SMEM)
F32 = jnp.float32
BF16 = jnp.bfloat16
HI = lax.Precision.HIGHEST
B = 32
T = 8


def dot(a, b, precision=None):
    return jnp.dot(a, b, precision=precision, preferred_element_type=F32)


def dot_nt(a, b, precision=None):
    return lax.dot_general(a, b, (((1,), (1,)), ((), ())), precision=precision, preferred_element_type=F32)


def dot_tn(a, b, precision=None):
    return lax.dot_general(a, b, (((0,), (0,)), ((), ())), precision=precision, preferred_element_type=F32)


def split3(v):
    hi = v.astype(BF16)
    rest = v - hi.astype(F32)
    mid = rest.astype(BF16)
    lo = (rest - mid.astype(F32)).astype(BF16)
    return hi, mid, lo


def dot_x3(a, b):
    ah = a.astype(BF16)
    al = (a - ah.astype(F32)).astype(BF16)
    bh = b.astype(BF16)
    bl = (b - bh.astype(F32)).astype(BF16)
    return dot(ah, bh) + (dot(ah, bl) + dot(al, bh))


def row_of(tile, i):
    return jnp.broadcast_to(tile[i : i + 1, :], tile.shape)


def inverse_factors(tiles, lane):
    n = len(tiles)
    sub = lax.broadcasted_iota(jnp.int32, (T, 128), 0)
    base = (lane // B) * B
    local = lane - base
    roots = []
    for t in range(n):
        cols = [[None] * n for _ in range(T)]
        for r in range(t, n):
            index = base + r * T + sub
            for i in range(T):
                cols[i][r] = jnp.take_along_axis(row_of(tiles[t], i), index, axis=1)
        block = (local >= t * T) & (local < (t + 1) * T)
        unit = jnp.where(local == sub + t * T, 1.0, 0.0)
        for r in range(t, n):
            tiles[r] = jnp.where(block, unit if r == t else 0.0, tiles[r])
        pivots = []
        for i in range(0, T, 2):
            a = row_of(cols[i][t], i)
            b = row_of(cols[i][t], i + 1)
            c = row_of(cols[i + 1][t], i + 1)
            det = a * c - b * b
            inv0 = 1.0 / a
            inv1 = a * (1.0 / det)
            ratio = b * inv0
            pivots += [a, det * inv0]
            row0, row1 = row_of(tiles[t], i), row_of(tiles[t], i + 1)
            f0 = row0 * inv0
            f1 = (row1 - ratio * row0) * inv1
            follow = []
            for m in range(i + 2, T):
                u0, u1 = row_of(cols[m][t], i), row_of(cols[m][t], i + 1)
                follow.append((u0 * inv0, (u1 - ratio * u0) * inv1))
            for r in range(t, n):
                c0 = cols[i][r]
                c1 = cols[i + 1][r] - ratio * c0
                if r == t:
                    c0 = jnp.where(sub > i, c0, 0.0)
                    c1 = jnp.where(sub > i + 1, c1, 0.0)
                tiles[r] = (tiles[r] - c0 * f0) - c1 * f1
                for m in range(i + 2, T):
                    h0, h1 = follow[m - i - 2]
                    cols[m][r] = (cols[m][r] - c0 * h0) - c1 * h1
        d = pivots[0]
        for i in range(1, T):
            d = jnp.where(sub == i, pivots[i], d)
        roots.append(lax.rsqrt(d))
    out = []
    for t in range(n):
        low = local <= (sub + t * T)
        out.append(jnp.where(low, tiles[t] * roots[t], 0.0))
    return out


def factor_body(nwin, gram_of_window, X):
    nb = 256 // B
    lane = lax.broadcasted_iota(jnp.int32, (T, 128), 1)
    lane_b = lax.broadcasted_iota(jnp.int32, (B, 128), 1)
    lane_r = lax.broadcasted_iota(jnp.int32, (B, 256), 1)
    rows_b = lax.broadcasted_iota(jnp.int32, (B, 256), 0)
    for w in range(nwin):
        g = gram_of_window(w)
        for k in range(nb):
            X[k, w * B : (w + 1) * B, :] = g[k * B : (k + 1) * B, :] + jnp.where(lane_r == rows_b + k * B, 255.0, 0.0)
    for k in range(nb):
        half = (k * B) // 128
        at = (k * B) % 128
        tiles = []
        for t in range(B // T):
            tile = None
            for w in range(nwin):
                part = X[k, w * B + t * T : w * B + (t + 1) * T, half * 128 : half * 128 + 128]
                shift = (w * B - at) % 128
                if shift:
                    part = pltpu.roll(part, shift, 1)
                tile = part if w == 0 else jnp.where(lane >= w * B, part, tile)
            tiles.append(tile)
        inv = jnp.concatenate(inverse_factors(tiles, lane), axis=0)
        lane_q = lax.broadcasted_iota(jnp.int32, (B, 256), 1)
        inside = (lane_q >= k * B) & (lane_q < (k + 1) * B)
        group = lane_b // B
        qs = []
        for w in range(nwin):
            spread = jnp.concatenate(
                [
                    jnp.take_along_axis(inv[t * T : (t + 1) * T], w * B + lane % B, axis=1)
                    for t in range(B // T)
                ],
                axis=0,
            )
            i1, i2, i3 = [piece.astype(F32) for piece in split3(spread)]
            first = jnp.where(group < 3, i1, i2)
            last = jnp.where(group == 0, i2, i3)
            r1, r2, r3 = split3(X[k, w * B : (w + 1) * B, :])
            left = jnp.concatenate([first, last], axis=1).astype(BF16)[:, : 6 * B]
            qw = dot(left, jnp.concatenate([r1, r2, r3, r1, r2, r1], axis=0))
            qw = jnp.where(inside, jnp.concatenate([spread, spread], axis=1), qw)
            qs.append(qw)
            X[k, w * B : (w + 1) * B, :] = jnp.where(lane_q < (k + 1) * B, qw, 0.0)
        if k + 1 == nb:
            continue
        for w in range(nwin):
            q1, q2, q3 = split3(qs[w])
            start = 128 * ((k + 1) * B // 128)
            left = jnp.concatenate([q1, q1, q1, q2, q2, q3], axis=0)[:, start:].T
            right = jnp.concatenate([q1, q2, q3, q1, q2, q1], axis=0)
            upd = dot(left[(k + 1) * B - start :], right).reshape(nb - k - 1, B, 256)
            below = X[k + 1 :, w * B : (w + 1) * B, :]
            X[k + 1 :, w * B : (w + 1) * B, :] = jnp.where(inside[None], 0.0, below) - upd


def factor_kernel(g_ref, scale_ref, far_ref, part_ref, own_ref, near_ref, X, Y, sem):
    fetch = pltpu.make_async_copy(far_ref, near_ref, sem)
    fetch.start()
    nz = g_ref.shape[0]
    nwin = scale_ref.shape[0]
    slots = 32
    packed = []
    for z in range(nz):
        both = g_ref[z, nwin * slots : nwin * slots + 8, :].astype(F32)
        packed.append((both[:, :128] + both[:, 128:]))
    columns = jnp.concatenate(packed, axis=0)
    columns = jnp.concatenate([columns, columns], axis=0).T

    def gram(w):
        parts = []
        for z in range(nz):
            y = g_ref[z, w * slots : (w + 1) * slots, :]
            Y[w, z * slots : (z + 1) * slots, :] = y
            col = columns[:slots, z * 8 + w : z * 8 + w + 1]
            parts.append(y.astype(F32) * col)
        weighted = jnp.concatenate(parts, axis=0)
        hi, mid, _ = split3(weighted)
        y = Y[w].T
        return dot(y, hi) + dot(y, mid)

    factor_body(nwin, gram, X)
    s = None
    for w in reversed(range(nwin)):
        x = X[:, w * B : (w + 1) * B, :].reshape(256, 256) * scale_ref[w]
        s = x if s is None else dot_x3(s, x)
        part_ref[w] = s
    own_ref[...] = pack(s).astype(BF16)
    fetch.wait()


def factor_call(g, scale, flat):
    nwin = scale.shape[0]
    return pl.pallas_call(
        factor_kernel,
        in_specs=[WHOLE, SCALARS, pl.BlockSpec(memory_space=pltpu.HBM)],
        out_specs=[WHOLE] * 3,
        out_shape=[
            jax.ShapeDtypeStruct((nwin, 256, 256), F32),
            PACKED,
            pltpu.VMEM(flat.shape, BF16),
        ],
        scratch_shapes=[
            pltpu.VMEM((256 // B, nwin * B, 256), F32),
            pltpu.VMEM((nwin, 256, 256), BF16),
            pltpu.SemaphoreType.DMA,
        ],
        compiler_params=pltpu.CompilerParams(vmem_limit_bytes=12 << 20),
        name="factor",
    )(g, scale, pltpu.with_memory_space_constraint(flat, pltpu.HBM))


def pick_kernel(cells_ref, counts_ref, lanes_ref, precision_ref, field_ref, out_ref, near, row_scr, sem):
    nwin, slots = cells_ref.shape
    width = field_ref.shape[2]

    def copy_of(w, k):
        first = pl.multiple_of(jnp.bitwise_and(cells_ref[w, k], width - 16), 16)
        return pltpu.make_async_copy(field_ref.at[w, 0, pl.ds(first, 16), :], near.at[w * slots + k], sem)

    for w in range(nwin):
        for k in range(slots):
            copy_of(w, k).start()
    row_scr[...] = jnp.zeros(row_scr.shape, F32)
    lane = lax.broadcasted_iota(jnp.int32, (1, slots), 1)
    for w in range(nwin):
        row_scr[w : w + 1, :slots] = jnp.where(lane < counts_ref[w], precision_ref[w : w + 1, :], 0.0)
    live = row_scr[...]
    high = live.astype(BF16)
    low = (live - high.astype(F32)).astype(BF16)
    tail = jnp.concatenate([high, low], axis=1)
    pltpu.make_async_copy(near, near, sem).wait()
    spot = lax.broadcasted_iota(jnp.int32, (slots * 16, slots), 0)
    slot = lax.broadcasted_iota(jnp.int32, (slots * 16, slots), 1)
    for w in range(nwin):
        within = jnp.bitwise_and(lanes_ref[w : w + 1, :], 15)
        chosen = jnp.where(spot == slot * 16 + within, 1.0, 0.0).astype(BF16)
        tiles = near[w * slots : (w + 1) * slots].reshape(slots * 16, near.shape[2])
        block = dot_tn(chosen, tiles).astype(BF16)
        for z in range(out_ref.shape[0]):
            out_ref[z, w * slots : (w + 1) * slots, :] = block
    for z in range(out_ref.shape[0]):
        out_ref[z, nwin * slots :, :] = tail


def pick_call(copies, anomalies, obs_cells, obs_counts, obs_precision):
    nwin, slots = obs_cells.shape
    members = anomalies.shape[3]
    return pl.pallas_call(
        pick_kernel,
        in_specs=[SCALARS, SCALARS, WHOLE, WHOLE, pl.BlockSpec(memory_space=pltpu.HBM)],
        out_specs=WHOLE,
        out_shape=jax.ShapeDtypeStruct((copies, nwin * slots + 8, members), BF16),
        scratch_shapes=[
            pltpu.VMEM((nwin * slots, 16, members), BF16),
            pltpu.VMEM((8, 128), F32),
            pltpu.SemaphoreType.DMA,
        ],
        name="pick",
    )(obs_cells, obs_counts, obs_cells, obs_precision, pltpu.with_memory_space_constraint(anomalies, pltpu.HBM))


def identity_bf16(n):
    return (lax.broadcasted_iota(jnp.int32, (n, n), 0) == lax.broadcasted_iota(jnp.int32, (n, n), 1)).astype(BF16)


def pack(s):
    h = 64
    top = jnp.concatenate([s[:h, :128][:, :h], s[128 : 128 + h, 128:][:, :h]], axis=1)
    return jnp.concatenate([top, s[h:128, :128], s[128 + h :, 128:], s[128:, :128]], axis=0)


def unpack(p):
    h = 64
    zero = jnp.zeros((h, h), p.dtype)
    first = jnp.concatenate([jnp.concatenate([p[:h, :h], zero], axis=1), p[h : 2 * h]], axis=0)
    last = jnp.concatenate([jnp.concatenate([p[:h, h:], zero], axis=1), p[2 * h : 3 * h]], axis=0)
    upper = jnp.concatenate([first, jnp.zeros((128, 128), p.dtype)], axis=1)
    lower = jnp.concatenate([p[3 * h :], last], axis=1)
    return jnp.concatenate([upper, lower], axis=0)


PACKED = jax.ShapeDtypeStruct((320, 128), jnp.bfloat16)


def pair_kernel(mine_ref, other_ref, both_ref):
    core = lax.axis_index("tm_2")
    mine, other = mine_ref[...].astype(F32), other_ref[...].astype(F32)
    first = unpack(jnp.where(core == 0, mine, other)).astype(BF16)
    second = unpack(jnp.where(core == 0, other, mine)).astype(BF16)
    both_ref[...] = pack(dot(second, first)).astype(BF16)


def ring_kernel(p0, p1, p2, p3, total_ref, later_ref, q):
    me = lax.axis_index("tm_1")
    for s, piece in enumerate((p0, p1, p2, p3)):
        q[lax.rem(me + s, 4)] = unpack(piece[...].astype(F32)).astype(BF16)
    high = dot(q[3], q[2])
    total_ref[...] = pack(dot_x3(high, dot(q[1], q[0]))).astype(BF16)
    later_ref[...] = high

    @pl.when(me == 0)
    def _():
        later_ref[...] = dot_x3(high, q[1].astype(F32))

    @pl.when(me == 2)
    def _():
        later_ref[...] = q[3].astype(F32)

    @pl.when(me == 3)
    def _():
        later_ref[...] = identity_bf16(256).astype(F32)


def inner_kernel(later_ref, other_ref, part_ref, out_ref, before):
    core = lax.axis_index("tm_2")
    before[...] = later_ref[...]

    @pl.when(core == 0)
    def _():
        before[...] = dot_x3(later_ref[...], unpack(other_ref[...].astype(F32)))

    for w in range(part_ref.shape[0]):
        out_ref[w] = dot_x3(before[...], part_ref[w])


def apply_kernel(p1, p2, p3, inner_ref, field_ref, out_ref, q, later, result, sems):
    me = lax.axis_index("tm_0")
    for s, piece in enumerate((p1, p2, p3)):
        q[lax.rem(me + s + 1, 4)] = unpack(piece[...].astype(F32)).astype(BF16)

    @pl.when(me == 0)
    def _():
        later[...] = dot_x3(dot(q[3], q[2]), q[1].astype(F32))

    @pl.when(me == 1)
    def _():
        later[...] = dot(q[3], q[2])

    @pl.when(me == 2)
    def _():
        later[...] = q[3].astype(F32)

    @pl.when(me == 3)
    def _():
        later[...] = identity_bf16(256).astype(F32)

    nwin, rows, _ = field_ref.shape
    copies = []
    for w in range(nwin):
        weights = dot_x3(later[...], inner_ref[w]).T.astype(BF16)
        for half in range(STEPS):
            span = pl.ds(half * (rows // STEPS), rows // STEPS)
            result[w, span, :] = dot(field_ref[w, span, :], weights).astype(BF16)
            copy = pltpu.make_async_copy(result.at[w, span], out_ref.at[w, span], sems.at[w, half])
            copy.start()
            copies.append(copy)
    for copy in copies:
        copy.wait()


STEPS = 2


def apply_call(pieces, inner, flat):
    nwin, rows, members = flat.shape
    return pl.pallas_call(
        apply_kernel,
        in_specs=[WHOLE] * 5,
        out_specs=pl.BlockSpec(memory_space=pltpu.HBM),
        out_shape=jax.ShapeDtypeStruct(flat.shape, BF16),
        scratch_shapes=[
            pltpu.VMEM((4, members, members), BF16),
            pltpu.VMEM((members, members), F32),
            pltpu.VMEM(flat.shape, BF16),
            pltpu.SemaphoreType.DMA((nwin, STEPS)),
        ],
        compiler_params=pltpu.CompilerParams(vmem_limit_bytes=24 << 20),
        name="apply",
    )(*pieces, inner, flat)


def simple_call(kernel, name, out_shape, scratch, *args):
    return pl.pallas_call(
        kernel,
        in_specs=[WHOLE] * len(args),
        out_specs=jax.tree.map(lambda _: WHOLE, out_shape),
        out_shape=out_shape,
        scratch_shapes=scratch,
        compiler_params=pltpu.CompilerParams(vmem_limit_bytes=8 << 20),
        name=name,
    )(*args)


def from_after(array, axis, shift):
    count = lax.axis_size(axis)
    return lax.ppermute(array, axis, [(i, (i - shift) % count) for i in range(count)])


def local(anomalies, obs_cells, obs_counts, obs_precision, inflation):
    nwin, _, cell_width, members = anomalies.shape
    square = (members, members)
    sent = pick_call(lax.axis_size("cell"), anomalies, obs_cells, obs_counts.reshape(nwin), obs_precision)
    flat = anomalies.reshape(nwin, 2 * cell_width, members)
    gathered = lax.all_to_all(sent, "cell", split_axis=0, concat_axis=0, tiled=True)
    part, own, near = factor_call(gathered, inflation * math.sqrt(members - 1.0), flat)
    other = from_after(own, "tm_2", 1)
    both = simple_call(pair_kernel, "pair", PACKED, [], own, other)
    pieces = [both] + [from_after(both, "tm_1", s) for s in (1, 2, 3)]
    total, later = simple_call(
        ring_kernel,
        "ring",
        [PACKED, jax.ShapeDtypeStruct(square, F32)],
        [pltpu.VMEM((4, *square), BF16)],
        *pieces,
    )
    after = [from_after(total, "tm_0", s) for s in (1, 2, 3)]
    inner = simple_call(
        inner_kernel,
        "inner",
        jax.ShapeDtypeStruct((nwin, *square), F32),
        [pltpu.VMEM(square, F32)],
        later,
        other,
        part,
    )
    return apply_call(after, inner, near).reshape(anomalies.shape)


def solution(mesh):
    torus = Mesh(
        mesh.devices.reshape(4, 4, 2, mesh.shape["cell"]), ("tm_0", "tm_1", "tm_2", "cell")
    )
    return jax.shard_map(
        local,
        mesh=torus,
        in_specs=(P(TM, None, "cell", None), P(TM, "cell"), P(TM, "cell"), P(TM, "cell"), P(TM)),
        out_specs=P(TM, None, "cell", None),
        check_vma=False,
    )
```

```python
import functools
import math
import jax
import jax.numpy as jnp
from jax import lax
from jax.experimental import pallas as pl
from jax.experimental.pallas import tpu as pltpu
from jax.sharding import Mesh
from jax.sharding import PartitionSpec as P

TM = ("tm_0", "tm_1", "tm_2")
WHOLE = pl.BlockSpec(memory_space=pltpu.VMEM)
SCALARS = pl.BlockSpec(memory_space=pltpu.SMEM)
F32 = jnp.float32
BF16 = jnp.bfloat16
HI = lax.Precision.HIGHEST
B = 32
T = 8


def dot(a, b, precision=None):
    return jnp.dot(a, b, precision=precision, preferred_element_type=F32)


def dot_nt(a, b, precision=None):
    return lax.dot_general(a, b, (((1,), (1,)), ((), ())), precision=precision, preferred_element_type=F32)


def dot_tn(a, b, precision=None):
    return lax.dot_general(a, b, (((0,), (0,)), ((), ())), precision=precision, preferred_element_type=F32)


def split3(v):
    hi = v.astype(BF16)
    rest = v - hi.astype(F32)
    mid = rest.astype(BF16)
    lo = (rest - mid.astype(F32)).astype(BF16)
    return hi, mid, lo


def dot_x3(a, b):
    ah = a.astype(BF16)
    al = (a - ah.astype(F32)).astype(BF16)
    bh = b.astype(BF16)
    bl = (b - bh.astype(F32)).astype(BF16)
    return dot(ah, bh) + (dot(ah, bl) + dot(al, bh))


def dot_nt_x3(a, b):
    ah = a.astype(BF16)
    al = (a - ah.astype(F32)).astype(BF16)
    bh = b.astype(BF16)
    bl = (b - bh.astype(F32)).astype(BF16)
    return dot_nt(ah, bh) + (dot_nt(ah, bl) + dot_nt(al, bh))


def row_of(tile, i):
    return jnp.broadcast_to(tile[i : i + 1, :], tile.shape)


def inverse_factors(tiles, lane):
    n = len(tiles)
    sub = lax.broadcasted_iota(jnp.int32, (T, 128), 0)
    base = (lane // B) * B
    local = lane - base
    roots = []
    for t in range(n):
        cols = [[None] * n for _ in range(T)]
        for r in range(t, n):
            index = base + r * T + sub
            for i in range(T):
                cols[i][r] = jnp.take_along_axis(row_of(tiles[t], i), index, axis=1)
        block = (local >= t * T) & (local < (t + 1) * T)
        unit = jnp.where(local == sub + t * T, 1.0, 0.0)
        for r in range(t, n):
            tiles[r] = jnp.where(block, unit if r == t else 0.0, tiles[r])
        pivots = []
        for i in range(0, T, 2):
            a = row_of(cols[i][t], i)
            b = row_of(cols[i][t], i + 1)
            c = row_of(cols[i + 1][t], i + 1)
            det = a * c - b * b
            inv0 = 1.0 / a
            inv1 = a * (1.0 / det)
            ratio = b * inv0
            pivots += [a, det * inv0]
            row0, row1 = row_of(tiles[t], i), row_of(tiles[t], i + 1)
            f0 = row0 * inv0
            f1 = (row1 - ratio * row0) * inv1
            follow = []
            for m in range(i + 2, T):
                u0, u1 = row_of(cols[m][t], i), row_of(cols[m][t], i + 1)
                follow.append((u0 * inv0, (u1 - ratio * u0) * inv1))
            for r in range(t, n):
                c0 = cols[i][r]
                c1 = cols[i + 1][r] - ratio * c0
                if r == t:
                    c0 = jnp.where(sub > i, c0, 0.0)
                    c1 = jnp.where(sub > i + 1, c1, 0.0)
                tiles[r] = (tiles[r] - c0 * f0) - c1 * f1
                for m in range(i + 2, T):
                    h0, h1 = follow[m - i - 2]
                    cols[m][r] = (cols[m][r] - c0 * h0) - c1 * h1
        d = pivots[0]
        for i in range(1, T):
            d = jnp.where(sub == i, pivots[i], d)
        roots.append(lax.rsqrt(d))
    out = []
    for t in range(n):
        low = local <= (sub + t * T)
        out.append(jnp.where(low, tiles[t] * roots[t], 0.0))
    return out


def factor_body(nwin, gram_of_window, X):
    nb = 256 // B
    lane = lax.broadcasted_iota(jnp.int32, (T, 128), 1)
    lane_b = lax.broadcasted_iota(jnp.int32, (B, 128), 1)
    lane_r = lax.broadcasted_iota(jnp.int32, (B, 256), 1)
    rows_b = lax.broadcasted_iota(jnp.int32, (B, 256), 0)
    for w in range(nwin):
        g = gram_of_window(w)
        for k in range(nb):
            X[k, w * B : (w + 1) * B, :] = g[k * B : (k + 1) * B, :] + jnp.where(lane_r == rows_b + k * B, 255.0, 0.0)
    for k in range(nb):
        half = (k * B) // 128
        at = (k * B) % 128
        tiles = []
        for t in range(B // T):
            tile = None
            for w in range(nwin):
                part = X[k, w * B + t * T : w * B + (t + 1) * T, half * 128 : half * 128 + 128]
                shift = (w * B - at) % 128
                if shift:
                    part = pltpu.roll(part, shift, 1)
                tile = part if w == 0 else jnp.where(lane >= w * B, part, tile)
            tiles.append(tile)
        inv = jnp.concatenate(inverse_factors(tiles, lane), axis=0)
        lane_q = lax.broadcasted_iota(jnp.int32, (B, 256), 1)
        inside = (lane_q >= k * B) & (lane_q < (k + 1) * B)
        group = lane_b // B
        qs = []
        for w in range(nwin):
            spread = jnp.concatenate(
                [
                    jnp.take_along_axis(inv[t * T : (t + 1) * T], w * B + lane % B, axis=1)
                    for t in range(B // T)
                ],
                axis=0,
            )
            i1, i2, i3 = [piece.astype(F32) for piece in split3(spread)]
            first = jnp.where(group < 3, i1, i2)
            last = jnp.where(group == 0, i2, i3)
            r1, r2, r3 = split3(X[k, w * B : (w + 1) * B, :])
            left = jnp.concatenate([first, last], axis=1).astype(BF16)[:, : 6 * B]
            qw = dot(left, jnp.concatenate([r1, r2, r3, r1, r2, r1], axis=0))
            qw = jnp.where(inside, jnp.concatenate([spread, spread], axis=1), qw)
            qs.append(qw)
            X[k, w * B : (w + 1) * B, :] = jnp.where(lane_q < (k + 1) * B, qw, 0.0)
        if k + 1 == nb:
            continue
        for w in range(nwin):
            q1, q2, q3 = split3(qs[w])
            start = 128 * ((k + 1) * B // 128)
            left = jnp.concatenate([q1, q1, q1, q2, q2, q3], axis=0)[:, start:].T
            right = jnp.concatenate([q1, q2, q3, q1, q2, q1], axis=0)
            upd = dot(left[(k + 1) * B - start :], right).reshape(nb - k - 1, B, 256)
            below = X[k + 1 :, w * B : (w + 1) * B, :]
            X[k + 1 :, w * B : (w + 1) * B, :] = jnp.where(inside[None], 0.0, below) - upd


def factor_kernel(g_ref, scale_ref, far_ref, part_ref, own_ref, near_ref, X, Y, sem):
    fetch = pltpu.make_async_copy(far_ref, near_ref, sem)
    fetch.start()
    nz = g_ref.shape[0]
    nwin = scale_ref.shape[0]
    slots = 32
    packed = []
    for z in range(nz):
        both = g_ref[z, nwin * slots : nwin * slots + 8, :].astype(F32)
        packed.append((both[:, :128] + both[:, 128:]))
    columns = jnp.concatenate(packed, axis=0)
    columns = jnp.concatenate([columns, columns], axis=0).T

    def gram(w):
        parts = []
        for z in range(nz):
            y = g_ref[z, w * slots : (w + 1) * slots, :]
            Y[w, z * slots : (z + 1) * slots, :] = y
            col = columns[:slots, z * 8 + w : z * 8 + w + 1]
            parts.append(y.astype(F32) * col)
        weighted = jnp.concatenate(parts, axis=0)
        hi, mid, _ = split3(weighted)
        y = Y[w].T
        return dot(y, hi) + dot(y, mid)

    factor_body(nwin, gram, X)
    s = None
    for w in reversed(range(nwin)):
        x = X[:, w * B : (w + 1) * B, :].reshape(256, 256) * scale_ref[w]
        s = x if s is None else dot_x3(s, x)
        part_ref[w] = s
    own_ref[...] = pack(s).astype(BF16)
    fetch.wait()


def factor_call(g, scale, flat):
    nwin = scale.shape[0]
    return pl.pallas_call(
        factor_kernel,
        in_specs=[WHOLE, SCALARS, pl.BlockSpec(memory_space=pltpu.HBM)],
        out_specs=[WHOLE] * 3,
        out_shape=[
            jax.ShapeDtypeStruct((nwin, 256, 256), F32),
            PACKED,
            pltpu.VMEM(flat.shape, BF16),
        ],
        scratch_shapes=[
            pltpu.VMEM((256 // B, nwin * B, 256), F32),
            pltpu.VMEM((nwin, 256, 256), BF16),
            pltpu.SemaphoreType.DMA,
        ],
        compiler_params=pltpu.CompilerParams(vmem_limit_bytes=12 << 20),
        name="factor",
    )(g, scale, pltpu.with_memory_space_constraint(flat, pltpu.HBM))


def pick_kernel(cells_ref, counts_ref, lanes_ref, precision_ref, field_ref, out_ref, near, row_scr, sem):
    nwin, slots = cells_ref.shape
    width = field_ref.shape[2]

    def copy_of(w, k):
        first = pl.multiple_of(jnp.bitwise_and(cells_ref[w, k], width - 16), 16)
        return pltpu.make_async_copy(field_ref.at[w, 0, pl.ds(first, 16), :], near.at[w * slots + k], sem)

    for w in range(nwin):
        for k in range(slots):
            copy_of(w, k).start()
    row_scr[...] = jnp.zeros(row_scr.shape, F32)
    lane = lax.broadcasted_iota(jnp.int32, (1, slots), 1)
    for w in range(nwin):
        row_scr[w : w + 1, :slots] = jnp.where(lane < counts_ref[w], precision_ref[w : w + 1, :], 0.0)
    live = row_scr[...]
    high = live.astype(BF16)
    low = (live - high.astype(F32)).astype(BF16)
    tail = jnp.concatenate([high, low], axis=1)
    pltpu.make_async_copy(near, near, sem).wait()
    spot = lax.broadcasted_iota(jnp.int32, (slots * 16, slots), 0)
    slot = lax.broadcasted_iota(jnp.int32, (slots * 16, slots), 1)
    for w in range(nwin):
        within = jnp.bitwise_and(lanes_ref[w : w + 1, :], 15)
        chosen = jnp.where(spot == slot * 16 + within, 1.0, 0.0).astype(BF16)
        tiles = near[w * slots : (w + 1) * slots].reshape(slots * 16, near.shape[2])
        block = dot_tn(chosen, tiles).astype(BF16)
        for z in range(out_ref.shape[0]):
            out_ref[z, w * slots : (w + 1) * slots, :] = block
    for z in range(out_ref.shape[0]):
        out_ref[z, nwin * slots :, :] = tail


def pick_call(copies, anomalies, obs_cells, obs_counts, obs_precision):
    nwin, slots = obs_cells.shape
    members = anomalies.shape[3]
    return pl.pallas_call(
        pick_kernel,
        in_specs=[SCALARS, SCALARS, WHOLE, WHOLE, pl.BlockSpec(memory_space=pltpu.HBM)],
        out_specs=WHOLE,
        out_shape=jax.ShapeDtypeStruct((copies, nwin * slots + 8, members), BF16),
        scratch_shapes=[
            pltpu.VMEM((nwin * slots, 16, members), BF16),
            pltpu.VMEM((8, 128), F32),
            pltpu.SemaphoreType.DMA,
        ],
        name="pick",
    )(obs_cells, obs_counts, obs_cells, obs_precision, pltpu.with_memory_space_constraint(anomalies, pltpu.HBM))


def identity_bf16(n):
    return (lax.broadcasted_iota(jnp.int32, (n, n), 0) == lax.broadcasted_iota(jnp.int32, (n, n), 1)).astype(BF16)


def pack(s):
    h = 64
    top = jnp.concatenate([s[:h, :128][:, :h], s[128 : 128 + h, 128:][:, :h]], axis=1)
    return jnp.concatenate([top, s[h:128, :128], s[128 + h :, 128:], s[128:, :128]], axis=0)


def unpack(p):
    h = 64
    zero = jnp.zeros((h, h), p.dtype)
    first = jnp.concatenate([jnp.concatenate([p[:h, :h], zero], axis=1), p[h : 2 * h]], axis=0)
    last = jnp.concatenate([jnp.concatenate([p[:h, h:], zero], axis=1), p[2 * h : 3 * h]], axis=0)
    upper = jnp.concatenate([first, jnp.zeros((128, 128), p.dtype)], axis=1)
    lower = jnp.concatenate([p[3 * h :], last], axis=1)
    return jnp.concatenate([upper, lower], axis=0)


PACKED = jax.ShapeDtypeStruct((320, 128), jnp.bfloat16)


def pair_kernel(mine_ref, other_ref, both_ref):
    core = lax.axis_index("tm_2")
    mine, other = mine_ref[...].astype(F32), other_ref[...].astype(F32)
    first = unpack(jnp.where(core == 0, mine, other)).astype(BF16)
    second = unpack(jnp.where(core == 0, other, mine)).astype(BF16)
    both_ref[...] = pack(dot(second, first)).astype(BF16)


def ring_kernel(p0, p1, p2, p3, total_ref, later_ref, q):
    me = lax.axis_index("tm_1")
    for s, piece in enumerate((p0, p1, p2, p3)):
        q[lax.rem(me + s, 4)] = unpack(piece[...].astype(F32)).astype(BF16)
    high = dot(q[3], q[2])
    total_ref[...] = pack(dot_x3(high, dot(q[1], q[0]))).astype(BF16)
    later_ref[...] = high

    @pl.when(me == 0)
    def _():
        later_ref[...] = dot_x3(high, q[1].astype(F32))

    @pl.when(me == 2)
    def _():
        later_ref[...] = q[3].astype(F32)

    @pl.when(me == 3)
    def _():
        later_ref[...] = identity_bf16(256).astype(F32)


def inner_kernel(later_ref, other_ref, part_ref, out_ref, before):
    core = lax.axis_index("tm_2")
    before[...] = later_ref[...]

    @pl.when(core == 0)
    def _():
        before[...] = dot_x3(later_ref[...], unpack(other_ref[...].astype(F32)))

    for w in range(part_ref.shape[0]):
        out_ref[w] = dot_x3(before[...], part_ref[w]).T


def apply_kernel(p1, p2, p3, inner_ref, field_ref, out_ref, q, later, result, sems):
    me = lax.axis_index("tm_0")
    for s, piece in enumerate((p1, p2, p3)):
        q[lax.rem(me + s + 1, 4)] = unpack(piece[...].astype(F32)).astype(BF16)

    @pl.when(me == 0)
    def _():
        later[...] = dot_x3(dot(q[3], q[2]), q[1].astype(F32))

    @pl.when(me == 1)
    def _():
        later[...] = dot(q[3], q[2])

    @pl.when(me == 2)
    def _():
        later[...] = q[3].astype(F32)

    @pl.when(me == 3)
    def _():
        later[...] = identity_bf16(256).astype(F32)

    nwin, rows, _ = field_ref.shape
    copies = []
    for w in range(nwin):
        weights = dot_nt_x3(inner_ref[w], later[...]).astype(BF16)
        for half in range(STEPS):
            span = pl.ds(half * (rows // STEPS), rows // STEPS)
            result[w, span, :] = dot(field_ref[w, span, :], weights).astype(BF16)
            copy = pltpu.make_async_copy(result.at[w, span], out_ref.at[w, span], sems.at[w, half])
            copy.start()
            copies.append(copy)
    for copy in copies:
        copy.wait()


STEPS = 4


def apply_call(pieces, inner, flat):
    nwin, rows, members = flat.shape
    return pl.pallas_call(
        apply_kernel,
        in_specs=[WHOLE] * 5,
        out_specs=pl.BlockSpec(memory_space=pltpu.HBM),
        out_shape=jax.ShapeDtypeStruct(flat.shape, BF16),
        scratch_shapes=[
            pltpu.VMEM((4, members, members), BF16),
            pltpu.VMEM((members, members), F32),
            pltpu.VMEM(flat.shape, BF16),
            pltpu.SemaphoreType.DMA((nwin, STEPS)),
        ],
        compiler_params=pltpu.CompilerParams(vmem_limit_bytes=24 << 20),
        name="apply",
    )(*pieces, inner, flat)


def simple_call(kernel, name, out_shape, scratch, *args):
    return pl.pallas_call(
        kernel,
        in_specs=[WHOLE] * len(args),
        out_specs=jax.tree.map(lambda _: WHOLE, out_shape),
        out_shape=out_shape,
        scratch_shapes=scratch,
        compiler_params=pltpu.CompilerParams(vmem_limit_bytes=8 << 20),
        name=name,
    )(*args)


def from_after(array, axis, shift):
    count = lax.axis_size(axis)
    return lax.ppermute(array, axis, [(i, (i - shift) % count) for i in range(count)])


def local(anomalies, obs_cells, obs_counts, obs_precision, inflation):
    nwin, _, cell_width, members = anomalies.shape
    square = (members, members)
    sent = pick_call(lax.axis_size("cell"), anomalies, obs_cells, obs_counts.reshape(nwin), obs_precision)
    flat = anomalies.reshape(nwin, 2 * cell_width, members)
    gathered = lax.all_to_all(sent, "cell", split_axis=0, concat_axis=0, tiled=True)
    part, own, near = factor_call(gathered, inflation * math.sqrt(members - 1.0), flat)
    other = from_after(own, "tm_2", 1)
    both = simple_call(pair_kernel, "pair", PACKED, [], own, other)
    pieces = [both] + [from_after(both, "tm_1", s) for s in (1, 2, 3)]
    total, later = simple_call(
        ring_kernel,
        "ring",
        [PACKED, jax.ShapeDtypeStruct(square, F32)],
        [pltpu.VMEM((4, *square), BF16)],
        *pieces,
    )
    after = [from_after(total, "tm_0", s) for s in (1, 2, 3)]
    inner = simple_call(
        inner_kernel,
        "inner",
        jax.ShapeDtypeStruct((nwin, *square), F32),
        [pltpu.VMEM(square, F32)],
        later,
        other,
        part,
    )
    return apply_call(after, inner, near).reshape(anomalies.shape)


def solution(mesh):
    torus = Mesh(
        mesh.devices.reshape(4, 4, 2, mesh.shape["cell"]), ("tm_0", "tm_1", "tm_2", "cell")
    )
    return jax.shard_map(
        local,
        mesh=torus,
        in_specs=(P(TM, None, "cell", None), P(TM, "cell"), P(TM, "cell"), P(TM, "cell"), P(TM)),
        out_specs=P(TM, None, "cell", None),
        check_vma=False,
    )
```
